32 devices in a mesh: groups: 2 (over y), ctx: 4 (over z), tp: 4 (over x, core).
Axes of the slice: x: 2, y: 2, z: 4, core: 2. Of those that a mesh axis runs over, the one named last changes fastest.
Arguments:
- queries: bfloat16 [1152, 8192], P(('groups', 'ctx'), 'tp'), parts along dimension 0, may hold values from -6 to 6
- keys: bfloat16 [1152, 1024], P(('groups', 'ctx'), 'tp'), parts along dimension 0, may hold values from -6 to 6
- values: bfloat16 [1152, 1024], P(('groups', 'ctx'), 'tp'), parts along dimension 0, may hold values from -6 to 6
- residual: bfloat16 [1152, 8192], P(('groups', 'ctx'), 'tp'), parts along dimension 0, may hold values from -4 to 4
- out_weight: bfloat16 [8192, 8192], P('tp', 'ctx'), may hold values from -0.0625 to 0.0625
- value_head: bfloat16 [8192], P('tp'), may hold values from -0.5 to 0.5
- segment_ids: int32 [1152], P(('groups', 'ctx')), parts along dimension 0, may hold values from 0 to 3, as said below
- positions: int32 [1152], P(('groups', 'ctx')), parts along dimension 0, may hold values from 0 to 251, as said below
- turn_ids: int32 [1152], P(('groups', 'ctx')), parts along dimension 0, may hold values from 0 to 15, as said below
Outputs:
- hidden_out: bfloat16 [1152, 8192], P(('groups', 'ctx'), 'tp'), parts along dimension 0
- turn_means: float32 [32], P('groups'), parts along dimension 0
The draws below stay inside these ranges and needn't reach their ends.
There are 2 independent parts, one for each index of `groups`. The reference program is written for one: setup_inputs(seed, part) draws one part's arguments, and reference() takes and returns one part's arrays. A program takes and returns all parts, laid end to end along the dimension named above; an argument that names none is the same for every part. Nothing has to cross between parts.
Inputs may be any that keep to these rules, and one draw needn't show every extreme that they name: `segment_ids`: in token order (the stored order reverted) segment ids never fall; the sequence holds 4 rollouts of 36 to 252 tokens, one of exactly 252. `positions`: A row's position is its token's offset from the first token of its rollout. `turn_ids`: A row's turn id is 4 times its segment id plus how many of its rollout's three turn starts lie at or before its position; turn starts lie at positions 1 to the rollout's length minus 1 and may coincide.
All inputs are finite; a program needn't handle non-finite values.
Results may differ from the reference program's by a relative error of at most 0.013.
Values may be sent and summed in bfloat16 or wider, within the bound.
A program may use at most 64 MiB of HBM per device.

```python
import math
import jax
import jax.numpy as jnp
from jax import lax

D = 8192
QUERY_HEADS = 64
KEY_VALUE_HEADS = 8
HEAD_SIZE = 128
TOK_DEV = 144
SEGS = 4
PACKED_TOKENS = 576
SEG_MEAN = 144
TURNS = 16
N_TP = 4


def layout(base_key):
    ctx_count = PACKED_TOKENS // TOK_DEV
    half_rows = TOK_DEV // 2
    row_index = jnp.arange(PACKED_TOKENS, dtype=jnp.int32)
    block_index = row_index // TOK_DEV
    inner_index = row_index % TOK_DEV
    token_of_row = jnp.where(inner_index < half_rows, block_index * half_rows + inner_index, (2 * ctx_count - 1 - block_index) * half_rows + inner_index - half_rows)
    segment_total = SEGS
    pair_total = segment_total // 2
    lengths_first = jax.random.randint(jax.random.fold_in(base_key, 1), (pair_total,), SEG_MEAN // 4, 7 * SEG_MEAN // 4 + 1)
    lengths_first = jnp.where(jnp.arange(pair_total) == 0, 7 * SEG_MEAN // 4, lengths_first)
    seg_lengths = jnp.concatenate([lengths_first, 2 * SEG_MEAN - lengths_first]).astype(jnp.int32)
    rest_order = jax.random.permutation(jax.random.fold_in(base_key, 3), segment_total - 1) + 1
    order = jnp.concatenate([jnp.zeros((1,), jnp.int32), rest_order.astype(jnp.int32)])
    seg_lengths = seg_lengths[order]
    seg_ends = jnp.cumsum(seg_lengths).astype(jnp.int32)
    seg_starts = seg_ends - seg_lengths
    token_index = jnp.arange(PACKED_TOKENS, dtype=jnp.int32)
    seg_of_token = jnp.sum((token_index[:, None] >= seg_ends[None, :]).astype(jnp.int32), axis=1)
    pos_of_token = token_index - seg_starts[seg_of_token]
    turn_cuts = jax.random.randint(jax.random.fold_in(base_key, 4), (segment_total, 3), 1, seg_lengths[:, None])
    turn_of_token = 4 * seg_of_token + jnp.sum((pos_of_token[:, None] >= turn_cuts[seg_of_token]).astype(jnp.int32), axis=1)
    return (token_of_row, seg_of_token, pos_of_token, turn_of_token)


def draw_segment_ids(base_key, part_index):
    token_of_row, seg_of_token, pos_of_token, turn_of_token = layout(base_key)
    return seg_of_token[token_of_row].astype(jnp.int32)


def draw_positions(base_key, part_index):
    token_of_row, seg_of_token, pos_of_token, turn_of_token = layout(base_key)
    return pos_of_token[token_of_row].astype(jnp.int32)


def draw_turn_ids(base_key, part_index):
    token_of_row, seg_of_token, pos_of_token, turn_of_token = layout(base_key)
    return turn_of_token[token_of_row].astype(jnp.int32)


def draw_queries(base_key, part_index):
    complete_shape = (PACKED_TOKENS, QUERY_HEADS * HEAD_SIZE)
    sampled_inputs = jax.random.truncated_normal(jax.random.fold_in(base_key, 11), -4.0, 4.0, complete_shape) * 1.5
    return sampled_inputs.astype(jnp.bfloat16)


def draw_keys(base_key, part_index):
    complete_shape = (PACKED_TOKENS, KEY_VALUE_HEADS * HEAD_SIZE)
    sampled_inputs = jax.random.truncated_normal(jax.random.fold_in(base_key, 12), -4.0, 4.0, complete_shape) * 1.5
    return sampled_inputs.astype(jnp.bfloat16)


def block_scale(key, extent, pieces, smallest, top_value):
    level = 1.0
    for dim, blocks in pieces:
        heights = jax.random.uniform(jax.random.fold_in(jax.random.fold_in(key, 6), dim), (blocks,), jnp.float32, smallest / len(pieces), top_value / len(pieces))
        level = level * jnp.repeat(jnp.exp(heights), extent[dim] // blocks).reshape((-1,) + (1,) * (len(extent) - 1 - dim))
    return level


def scatter_about(rng, dims, scale, bound, cuts=(), held_as=jnp.bfloat16):
    drawn = jax.random.normal(rng, dims, jnp.float32) * scale
    if len(cuts) > 0:
        drawn = block_scale(rng, dims, cuts, -0.22, 0.18) * drawn
    return jnp.clip(drawn, min=-bound, max=bound).astype(held_as)


def setup_inputs(seed: int = 0, part: int = 0) -> dict:
    key_of = jax.random.split(jax.random.key(seed), 10)
    part_keys = jax.random.split(jax.random.fold_in(key_of[9], part), 10)
    return {
        "queries": draw_queries(jax.random.fold_in(jax.random.fold_in(key_of[9], part), 71), part),
        "keys": draw_keys(jax.random.fold_in(jax.random.fold_in(key_of[9], part), 71), part),
        "values": scatter_about(part_keys[2], (PACKED_TOKENS, KEY_VALUE_HEADS * HEAD_SIZE), 1.0, 6.0, ((0, 4), (1, 4))),
        "residual": scatter_about(part_keys[3], (PACKED_TOKENS, D), 0.5, 4.0, ((0, 4), (1, 4))),
        "out_weight": scatter_about(key_of[4], (QUERY_HEADS * HEAD_SIZE, D), (QUERY_HEADS * HEAD_SIZE) ** -0.5, 0.0625, ((0, 4), (1, 4))),
        "value_head": scatter_about(key_of[5], (D,), (D // 64) ** -0.5, 0.5, ((0, 4),)),
        "segment_ids": draw_segment_ids(jax.random.fold_in(jax.random.fold_in(key_of[9], part), 71), part),
        "positions": draw_positions(jax.random.fold_in(jax.random.fold_in(key_of[9], part), 71), part),
        "turn_ids": draw_turn_ids(jax.random.fold_in(jax.random.fold_in(key_of[9], part), 71), part),
    }


def reference(queries, keys, values, residual, out_weight, value_head, segment_ids, positions, turn_ids):
    sequence_length = queries.shape[0]
    query_head_group = QUERY_HEADS // KEY_VALUE_HEADS
    tile_row_count = math.gcd(sequence_length, 128)
    score_scale = 1.0 / math.sqrt(HEAD_SIZE)
    key_head_rows = keys.reshape(sequence_length, KEY_VALUE_HEADS, HEAD_SIZE).astype(jnp.float32)
    value_head_rows = values.reshape(sequence_length, KEY_VALUE_HEADS, HEAD_SIZE).astype(jnp.float32)

    def one_block(block_index):
        first_row = block_index * tile_row_count
        query_tile = lax.dynamic_slice_in_dim(queries, first_row, tile_row_count, 0)
        query_tile = query_tile.reshape(tile_row_count, KEY_VALUE_HEADS, query_head_group, HEAD_SIZE).astype(jnp.float32)
        seg_block = lax.dynamic_slice_in_dim(segment_ids, first_row, tile_row_count, 0)
        pos_block = lax.dynamic_slice_in_dim(positions, first_row, tile_row_count, 0)
        allowed = (seg_block[:, None] == segment_ids[None, :]) & (positions[None, :] <= pos_block[:, None])
        scores = jnp.einsum('qhgd,khd->hgqk', query_tile, key_head_rows) * score_scale
        scores = jnp.where(allowed, scores, -1e+30)
        row_max = lax.optimization_barrier(jnp.max(scores, axis=-1, keepdims=True))
        weights = jnp.where(allowed, jnp.exp(scores - row_max), 0.0)
        denominator = lax.optimization_barrier(jnp.sum(weights, axis=-1))
        rounded = lax.optimization_barrier(weights.astype(jnp.bfloat16)).astype(jnp.float32)
        numerator = jnp.einsum('hgqk,khd->hgqd', rounded, value_head_rows)
        outcome = numerator / denominator[..., None]
        return outcome.transpose(2, 0, 1, 3).reshape(tile_row_count, QUERY_HEADS * HEAD_SIZE).astype(jnp.bfloat16)
    attention = lax.map(one_block, jnp.arange(sequence_length // tile_row_count, dtype=jnp.int32))
    attention = attention.reshape(sequence_length, QUERY_HEADS * HEAD_SIZE)
    group_cols = QUERY_HEADS * HEAD_SIZE // N_TP
    projection = jnp.zeros((sequence_length, D), jnp.float32)
    for tp_group in range(N_TP):
        lower = tp_group * group_cols
        upper = lower + group_cols
        partial_term = jnp.dot(attention[:, lower:upper], out_weight[lower:upper], preferred_element_type=jnp.float32)
        projection = projection + lax.optimization_barrier(partial_term.astype(jnp.bfloat16)).astype(jnp.float32)
    hidden_out = (residual.astype(jnp.float32) + projection).astype(jnp.bfloat16)
    token_score = jnp.dot(hidden_out, value_head, preferred_element_type=jnp.float32)
    one_hot = (turn_ids[:, None] == jnp.arange(TURNS, dtype=jnp.int32)[None, :]).astype(jnp.float32)
    turn_sum = jnp.dot(token_score, one_hot, precision=lax.Precision.HIGHEST)
    turn_count = lax.optimization_barrier(jnp.sum(one_hot, axis=0))
    turn_means = turn_sum / jnp.maximum(turn_count, 1.0)
    return (hidden_out, turn_means)
```

```python
import functools
import math

import jax
import jax.numpy as jnp
from jax import lax
from jax.experimental import pallas as pl
from jax.experimental.pallas import tpu as pltpu
from jax.sharding import PartitionSpec as P

HEAD_SIZE = 128
TURNS = 16


def shards(
    queries, keys, values, residual, out_weight, value_head, segment_ids, positions, turn_ids
):
    tok_rows = queries.shape[0]
    kv_heads = keys.shape[1] // HEAD_SIZE
    query_head_group = queries.shape[1] // keys.shape[1]
    query_rows = query_head_group * tok_rows
    score_scale = 1.0 / math.sqrt(HEAD_SIZE)
    grouped = (
        queries.reshape(tok_rows, kv_heads, query_head_group, HEAD_SIZE)
        .transpose(1, 2, 0, 3)
        .reshape(kv_heads, query_rows, HEAD_SIZE)
    )
    seg_rows = jnp.tile(segment_ids, query_head_group)
    pos_rows = jnp.tile(positions, query_head_group)

    def update(running, key_block, value_block, seg_block, pos_block):
        allowed = (seg_rows[:, None] == seg_block[None, :]) & (
            pos_block[None, :] <= pos_rows[:, None]
        )
        numerator, row_max, denominator = running
        scores = (
            jnp.einsum("hqd,khd->hqk", grouped, key_block, preferred_element_type=jnp.float32)
            * score_scale
        )
        scores = jnp.where(allowed[None], scores, -1e30)
        new_max = jnp.maximum(row_max, jnp.max(scores, axis=2))
        weights = jnp.where(allowed[None], jnp.exp(scores - new_max[..., None]), 0.0)
        factor = jnp.exp(row_max - new_max)
        denominator = denominator * factor + jnp.sum(weights, axis=2)
        product = jnp.einsum(
            "hqk,khd->hqd",
            weights.astype(jnp.bfloat16),
            value_block,
            preferred_element_type=jnp.float32,
        )
        numerator = numerator * factor[..., None] + product
        return (numerator, new_max, denominator)

    initial = (
        jnp.zeros((kv_heads, query_rows, HEAD_SIZE), jnp.float32),
        jnp.full((kv_heads, query_rows), -1e30, jnp.float32),
        jnp.zeros((kv_heads, query_rows), jnp.float32),
    )
    running = initial
    key_piece = lax.all_gather(keys, "ctx", axis=0, tiled=True)
    value_piece = lax.all_gather(values, "ctx", axis=0, tiled=True)
    seg_piece = lax.all_gather(segment_ids, "ctx", axis=0, tiled=True)
    pos_piece = lax.all_gather(positions, "ctx", axis=0, tiled=True)
    row_count = key_piece.shape[0]
    key_piece = key_piece.reshape(row_count, kv_heads, HEAD_SIZE)
    value_piece = value_piece.reshape(row_count, kv_heads, HEAD_SIZE)
    block_width = math.gcd(row_count, 512)
    block_steps = row_count // block_width
    stacked = (
        key_piece.reshape(block_steps, block_width, kv_heads, HEAD_SIZE),
        value_piece.reshape(block_steps, block_width, kv_heads, HEAD_SIZE),
        seg_piece.reshape(block_steps, block_width),
        pos_piece.reshape(block_steps, block_width),
    )

    def block_step(running_state, block_set):
        return (update(running_state, block_set[0], block_set[1], block_set[2], block_set[3]), None)

    running, _ = lax.scan(block_step, running, stacked)
    numerator, row_max, denominator = running
    attention = (numerator / denominator[..., None]).reshape(
        kv_heads, query_head_group, tok_rows, HEAD_SIZE
    )
    attention = (
        attention.transpose(2, 0, 1, 3)
        .reshape(tok_rows, kv_heads * query_head_group * HEAD_SIZE)
        .astype(jnp.bfloat16)
    )
    partial_value = jnp.dot(
        lax.all_gather(attention, "ctx", axis=0, tiled=True),
        out_weight,
        preferred_element_type=jnp.float32,
    ).astype(jnp.bfloat16)
    term_rows = lax.all_to_all(
        partial_value, "ctx", split_axis=0, concat_axis=1, tiled=True
    ).astype(jnp.float32)
    summed = lax.psum_scatter(
        term_rows.astype(jnp.bfloat16), "tp", scatter_dimension=1, tiled=True
    ).astype(jnp.float32)
    hidden_out = (residual.astype(jnp.float32) + summed).astype(jnp.bfloat16)
    token_score = jnp.dot(hidden_out, value_head, preferred_element_type=jnp.float32)
    one_hot = (turn_ids[:, None] == jnp.arange(TURNS, dtype=jnp.int32)[None, :]).astype(jnp.float32)
    local_sum = jnp.dot(token_score, one_hot, precision=lax.Precision.HIGHEST)
    local_count = jnp.where(lax.axis_index("tp") == 0, jnp.sum(one_hot, axis=0), 0.0)
    totals, counts = lax.psum((local_sum, local_count), ("ctx", "tp"))
    turn_means = totals / jnp.maximum(counts, 1.0)
    return (hidden_out, turn_means)


MESH = pl.DeviceIdType.MESH
F32 = jnp.float32
BF16 = jnp.bfloat16


def kernel(
    dims, q_ref, k_ref, v_ref, code_ref, qcode_ref, tid_ref, vh_ref, res_hbm, w_hbm,
    out_ref, mean_ref,
    kg, vg, cg, ccol, qs, ot, att, wv, part, rs, red, fin, resv, tot,
    k_send, v_send, c_send, k_recv, v_recv, c_recv, att_send, att_recv,
    rs_send, rs_recv, fin_send, fin_recv, tot_send, tot_recv, w_sem, res_sem,
):
    n, tn, rows, groups, per, cb, lanes = dims
    c = lax.axis_index("ctx")
    t = lax.axis_index("tp")
    keys_all = n * rows
    half = per * HEAD_SIZE
    scale = 1.0 / math.sqrt(HEAD_SIZE)

    def w_copy(i):
        return pltpu.make_async_copy(
            w_hbm.at[:, pl.ds(pl.multiple_of(i * cb, 128), cb)], wv.at[i], w_sem.at[i]
        )

    res_copy = pltpu.make_async_copy(res_hbm, resv, res_sem)
    for i in range(tn):
        w_copy(i).start()
    res_copy.start()

    barrier = pltpu.get_barrier_semaphore()

    def greet(i, _):
        other = lax.rem(c * tn + t + 1 + i, n * tn)
        pl.semaphore_signal(
            barrier, inc=1, device_id={"ctx": other // tn, "tp": lax.rem(other, tn)},
            device_id_type=MESH,
        )
        return 0

    lax.fori_loop(0, n * tn - 1, greet, 0)
    kg[c] = k_ref[...]
    vg[c] = v_ref[...]
    cg[c] = code_ref[...]
    pl.semaphore_wait(barrier, n * tn - 1)

    def kv_copies(s, d, own):
        dev = {"ctx": c + 1 - 2 * d}
        out = []
        for src, buf, snd, rcv in (
            (k_ref, kg, k_send, k_recv),
            (v_ref, vg, v_send, v_recv),
            (code_ref, cg, c_send, c_recv),
        ):
            out.append(
                pltpu.make_async_remote_copy(
                    src_ref=src if own else buf.at[s], dst_ref=buf.at[s],
                    send_sem=snd.at[d, s], recv_sem=rcv.at[s],
                    device_id=dev, device_id_type=MESH,
                )
            )
        return out

    def att_copy(s, g, d):
        return pltpu.make_async_remote_copy(
            src_ref=att.at[s, g], dst_ref=att.at[s, g],
            send_sem=att_send.at[d, s, g], recv_sem=att_recv.at[s, g],
            device_id={"ctx": c + 1 - 2 * d}, device_id_type=MESH,
        )

    def rs_copy(s, i):
        return pltpu.make_async_remote_copy(
            src_ref=part.at[s, i], dst_ref=rs.at[s, t],
            send_sem=rs_send.at[s, i], recv_sem=rs_recv.at[s, t],
            device_id={"tp": i}, device_id_type=MESH,
        )

    def rs_arrival(s, i):
        return pltpu.make_async_remote_copy(
            src_ref=part.at[s, i], dst_ref=rs.at[s, i],
            send_sem=rs_send.at[s, i], recv_sem=rs_recv.at[s, i],
            device_id={"tp": i}, device_id_type=MESH,
        )

    def fin_copy(s):
        return pltpu.make_async_remote_copy(
            src_ref=red.at[s], dst_ref=fin.at[t],
            send_sem=fin_send.at[s], recv_sem=fin_recv.at[t],
            device_id={"ctx": s, "tp": c}, device_id_type=MESH,
        )

    def fin_arrival(i):
        return pltpu.make_async_remote_copy(
            src_ref=red.at[0], dst_ref=fin.at[i],
            send_sem=fin_send.at[0], recv_sem=fin_recv.at[i],
            device_id={"ctx": t, "tp": i}, device_id_type=MESH,
        )

    def goes(s, d):
        if d == 0:
            return (s <= c) & (c < n - 1)
        return (s >= c) & (c > 0)

    for d in range(2):
        @pl.when(goes(c, d))
        def _():
            for cp in kv_copies(c, d, True):
                cp.start()

    for g in range(groups):
        for h in range(per):
            col = (g * per + h) * HEAD_SIZE
            qs[g, h * rows:(h + 1) * rows, :] = q_ref[:, col:col + HEAD_SIZE]

    def order(m):
        low = c
        high = n - 1 - c
        both = jnp.minimum(low, high)
        near = jnp.where(lax.rem(m, 2) == 1, c - (m + 1) // 2, c + m // 2)
        far = jnp.where(low > high, c - (m - high), c + (m - low))
        return jnp.where(m <= 2 * both, near, far)

    def kv_step(m, _):
        s = order(m)
        for cp in kv_copies(s, 0, False):
            cp.wait_recv()
        for d in range(2):
            @pl.when(goes(s, d))
            def _():
                for cp in kv_copies(s, d, False):
                    cp.start()
        return 0

    lax.fori_loop(1, n, kv_step, 0)

    for s in range(n):
        block = jnp.broadcast_to(cg[s, 0:1, :], (128, cg.shape[2]))
        ccol[s] = block.T[:rows, 0:1]

    for g in range(groups):
        sl = slice(g * HEAD_SIZE, (g + 1) * HEAD_SIZE)

        def score_step(i, _):
            span = pl.ds(pl.multiple_of(i * lanes, 128), lanes)
            keys = kg[:, :, sl].reshape(keys_all, HEAD_SIZE)
            vals = vg[:, :, sl].reshape(keys_all, HEAD_SIZE)
            s = lax.dot_general(
                keys, qs[g, span, :], (((1,), (1,)), ((), ())), preferred_element_type=F32
            ) * scale
            cj = ccol[...].reshape(keys_all, 1)
            allowed = (cj <= qcode_ref[0:1, span]) & (cj >= qcode_ref[1:2, span])
            s = jnp.where(allowed, s, -1e30)
            top = jnp.max(s, axis=0, keepdims=True)
            p = jnp.where(allowed, jnp.exp(s - top), 0.0)
            den = jnp.sum(p, axis=0, keepdims=True)
            o = lax.dot_general(
                vals, p.astype(BF16), (((0,), (0,)), ((), ())), preferred_element_type=F32
            )
            ot[span, :] = (o / den).T.astype(BF16)
            return 0

        lax.fori_loop(0, per * rows // lanes, score_step, 0)
        for h in range(per):
            att[c, g, :, h * HEAD_SIZE:(h + 1) * HEAD_SIZE] = ot[h * rows:(h + 1) * rows, :]
        for d in range(2):
            @pl.when(goes(c, d))
            def _():
                att_copy(c, g, d).start()

    for i in range(tn):
        w_copy(i).wait()

    def reduce_send(s):
        total = None
        for i in range(tn):
            @pl.when(t != i)
            def _():
                rs_arrival(s, i).wait_recv()
        for i in range(tn):
            term = rs[s, i].astype(F32)
            total = term if total is None else total + term
        summed = total.astype(BF16)
        mine = (s == c) & (t == c)

        @pl.when(mine)
        def _():
            fin[t] = summed

        @pl.when(jnp.logical_not(mine))
        def _():
            red[s] = summed
            fin_copy(s).start()

    def step(m, _):
        @pl.when(m < n)
        def _():
            s = order(m)

            @pl.when(m > 0)
            def _():
                for g in range(groups):
                    att_copy(s, g, 0).wait_recv()
                    for d in range(2):
                        @pl.when(goes(s, d))
                        def _():
                            att_copy(s, g, d).start()

        @pl.when(m > 0)
        def _():
            reduce_send(order(m - 1))

        @pl.when(m < n)
        def _():
            s = order(m)

            def column(j, _):
                i = lax.rem(t + 1 + j, tn)
                acc = None
                for g in range(groups):
                    prod = jnp.dot(
                        att[s, g], wv[i, g * half:(g + 1) * half, :],
                        preferred_element_type=F32,
                    )
                    acc = prod if acc is None else acc + prod
                value = acc.astype(BF16)

                @pl.when(i == t)
                def _():
                    rs[s, t] = value

                @pl.when(i != t)
                def _():
                    part[s, i] = value
                    rs_copy(s, i).start()

                return 0

            lax.fori_loop(0, tn, column, 0)

        return 0

    lax.fori_loop(0, n + 1, step, 0)

    res_copy.wait()
    score = jnp.zeros((rows, 1), F32)
    for i in range(tn):
        @pl.when(jnp.logical_not((c == t) & (t == i)))
        def _():
            fin_arrival(i).wait_recv()
        span = slice(i * cb, (i + 1) * cb)
        hidden = (resv[:, span].astype(F32) + fin[i].astype(F32)).astype(BF16)
        out_ref[:, span] = hidden
        score = score + jnp.sum(
            hidden.astype(F32) * vh_ref[:, span].astype(F32), axis=1, keepdims=True
        )
    turn = lax.broadcasted_iota(jnp.int32, (rows, 128), 1)
    hot = (tid_ref[...] == turn).astype(F32)
    sums = jnp.sum(hot * score, axis=0, keepdims=True)
    counts = jnp.sum(hot, axis=0, keepdims=True)
    counts = counts * jnp.where(t == 0, 1.0, 0.0)
    row = lax.broadcasted_iota(jnp.int32, (8, 128), 0)
    me = c * tn + t
    tot[me] = jnp.where(row == 0, sums, jnp.where(row == 1, counts, 0.0))

    def tot_copy(j):
        other = lax.rem(me + j, n * tn)
        return pltpu.make_async_remote_copy(
            src_ref=tot.at[me], dst_ref=tot.at[me],
            send_sem=tot_send.at[other], recv_sem=tot_recv.at[me],
            device_id={"ctx": other // tn, "tp": lax.rem(other, tn)}, device_id_type=MESH,
        )

    def tot_arrival(j):
        other = lax.rem(me + j, n * tn)
        return pltpu.make_async_remote_copy(
            src_ref=tot.at[me], dst_ref=tot.at[other],
            send_sem=tot_send.at[other], recv_sem=tot_recv.at[other],
            device_id={"ctx": other // tn, "tp": lax.rem(other, tn)}, device_id_type=MESH,
        )

    def tot_start(j, _):
        tot_copy(j).start()
        return 0

    lax.fori_loop(1, n * tn, tot_start, 0)

    def drain(s, _):
        for d in range(2):
            @pl.when(goes(s, d))
            def _():
                for cp in kv_copies(s, d, False):
                    cp.wait_send()
                for g in range(groups):
                    att_copy(s, g, d).wait_send()
        for i in range(tn):
            @pl.when(t != i)
            def _():
                rs_copy(s, i).wait_send()

        @pl.when(jnp.logical_not((s == c) & (t == c)))
        def _():
            fin_copy(s).wait_send()

        return 0

    lax.fori_loop(0, n, drain, 0)

    def tot_wait(j, _):
        tot_arrival(j).wait_recv()
        tot_copy(j).wait_send()
        return 0

    lax.fori_loop(1, n * tn, tot_wait, 0)
    whole = jnp.sum(tot[...], axis=0)
    mean_ref[...] = whole[0:1, :TURNS] / jnp.maximum(whole[1:2, :TURNS], 1.0)


def fused(
    n, tn, queries, keys, values, residual, out_weight, value_head, segment_ids, positions, turn_ids
):
    rows, width = queries.shape
    groups = keys.shape[1] // HEAD_SIZE
    per = width // keys.shape[1]
    cols = out_weight.shape[1]
    cb = cols // tn
    lanes = next(x for x in (384, 256, 128) if (per * rows) % x == 0)
    low = segment_ids * (n * rows)
    code = low + positions
    padded = -(-rows // 128) * 128
    code_block = jnp.broadcast_to(jnp.pad(code, (0, padded - rows))[None, :], (8, padded))
    qcode = jnp.stack([jnp.tile(code, per), jnp.tile(low, per)])
    dims = (n, tn, rows, groups, per, cb, lanes)
    vmem = pl.BlockSpec(memory_space=pltpu.VMEM)
    hbm = pl.BlockSpec(memory_space=pl.ANY)
    dma = pltpu.SemaphoreType.DMA
    out, means = pl.pallas_call(
        functools.partial(kernel, dims),
        out_shape=(
            jax.ShapeDtypeStruct((rows, cols), BF16),
            jax.ShapeDtypeStruct((1, TURNS), F32),
        ),
        in_specs=[vmem] * 7 + [hbm] * 2,
        out_specs=(vmem, vmem),
        scratch_shapes=[
            pltpu.VMEM((n, rows, groups * HEAD_SIZE), BF16),
            pltpu.VMEM((n, rows, groups * HEAD_SIZE), BF16),
            pltpu.VMEM((n, 8, padded), jnp.int32),
            pltpu.VMEM((n, rows, 1), jnp.int32),
            pltpu.VMEM((groups, per * rows, HEAD_SIZE), BF16),
            pltpu.VMEM((per * rows, HEAD_SIZE), BF16),
            pltpu.VMEM((n, groups, rows, per * HEAD_SIZE), BF16),
            pltpu.VMEM((tn, width, cb), BF16),
            pltpu.VMEM((n, tn, rows, cb), BF16),
            pltpu.VMEM((n, tn, rows, cb), BF16),
            pltpu.VMEM((n, rows, cb), BF16),
            pltpu.VMEM((tn, rows, cb), BF16),
            pltpu.VMEM((rows, cols), BF16),
            pltpu.VMEM((n * tn, 8, 128), F32),
            dma((2, n)), dma((2, n)), dma((2, n)),
            dma((n,)), dma((n,)), dma((n,)),
            dma((2, n, groups)), dma((n, groups)),
            dma((n, tn)), dma((n, tn)),
            dma((n,)), dma((tn,)),
            dma((n * tn,)), dma((n * tn,)),
            dma((tn,)), dma(()),
        ],
        compiler_params=pltpu.CompilerParams(
            collective_id=0, has_side_effects=True, vmem_limit_bytes=56 * 1024 * 1024
        ),
    )(
        queries, keys, values, code_block, qcode, turn_ids.reshape(rows, 1),
        value_head.reshape(1, -1), residual, out_weight,
    )
    return out, means.reshape(TURNS)


def body(n, tn, *args):
    queries, weight = args[0], args[4]
    rows = queries.shape[0]
    fits = n == tn and rows % 16 == 0 and weight.shape[1] % (128 * tn) == 0
    if fits:
        return fused(n, tn, *args)
    return shards(*args)


def solution(mesh):
    return jax.shard_map(
        functools.partial(body, mesh.shape["ctx"], mesh.shape["tp"]),
        mesh=mesh,
        in_specs=(
            P(("groups", "ctx"), "tp"),
            P(("groups", "ctx"), "tp"),
            P(("groups", "ctx"), "tp"),
            P(("groups", "ctx"), "tp"),
            P("tp", "ctx"),
            P("tp"),
            P(("groups", "ctx")),
            P(("groups", "ctx")),
            P(("groups", "ctx")),
        ),
        out_specs=(P(("groups", "ctx"), "tp"), P("groups")),
        check_vma=False,
    )
```

```python
import functools
import math

import jax
import jax.numpy as jnp
from jax import lax
from jax.experimental import pallas as pl
from jax.experimental.pallas import tpu as pltpu
from jax.sharding import PartitionSpec as P

HEAD_SIZE = 128
TURNS = 16


def shards(
    queries, keys, values, residual, out_weight, value_head, segment_ids, positions, turn_ids
):
    tok_rows = queries.shape[0]
    kv_heads = keys.shape[1] // HEAD_SIZE
    query_head_group = queries.shape[1] // keys.shape[1]
    query_rows = query_head_group * tok_rows
    score_scale = 1.0 / math.sqrt(HEAD_SIZE)
    grouped = (
        queries.reshape(tok_rows, kv_heads, query_head_group, HEAD_SIZE)
        .transpose(1, 2, 0, 3)
        .reshape(kv_heads, query_rows, HEAD_SIZE)
    )
    seg_rows = jnp.tile(segment_ids, query_head_group)
    pos_rows = jnp.tile(positions, query_head_group)

    def update(running, key_block, value_block, seg_block, pos_block):
        allowed = (seg_rows[:, None] == seg_block[None, :]) & (
            pos_block[None, :] <= pos_rows[:, None]
        )
        numerator, row_max, denominator = running
        scores = (
            jnp.einsum("hqd,khd->hqk", grouped, key_block, preferred_element_type=jnp.float32)
            * score_scale
        )
        scores = jnp.where(allowed[None], scores, -1e30)
        new_max = jnp.maximum(row_max, jnp.max(scores, axis=2))
        weights = jnp.where(allowed[None], jnp.exp(scores - new_max[..., None]), 0.0)
        factor = jnp.exp(row_max - new_max)
        denominator = denominator * factor + jnp.sum(weights, axis=2)
        product = jnp.einsum(
            "hqk,khd->hqd",
            weights.astype(jnp.bfloat16),
            value_block,
            preferred_element_type=jnp.float32,
        )
        numerator = numerator * factor[..., None] + product
        return (numerator, new_max, denominator)

    initial = (
        jnp.zeros((kv_heads, query_rows, HEAD_SIZE), jnp.float32),
        jnp.full((kv_heads, query_rows), -1e30, jnp.float32),
        jnp.zeros((kv_heads, query_rows), jnp.float32),
    )
    running = initial
    key_piece = lax.all_gather(keys, "ctx", axis=0, tiled=True)
    value_piece = lax.all_gather(values, "ctx", axis=0, tiled=True)
    seg_piece = lax.all_gather(segment_ids, "ctx", axis=0, tiled=True)
    pos_piece = lax.all_gather(positions, "ctx", axis=0, tiled=True)
    row_count = key_piece.shape[0]
    key_piece = key_piece.reshape(row_count, kv_heads, HEAD_SIZE)
    value_piece = value_piece.reshape(row_count, kv_heads, HEAD_SIZE)
    block_width = math.gcd(row_count, 512)
    block_steps = row_count // block_width
    stacked = (
        key_piece.reshape(block_steps, block_width, kv_heads, HEAD_SIZE),
        value_piece.reshape(block_steps, block_width, kv_heads, HEAD_SIZE),
        seg_piece.reshape(block_steps, block_width),
        pos_piece.reshape(block_steps, block_width),
    )

    def block_step(running_state, block_set):
        return (update(running_state, block_set[0], block_set[1], block_set[2], block_set[3]), None)

    running, _ = lax.scan(block_step, running, stacked)
    numerator, row_max, denominator = running
    attention = (numerator / denominator[..., None]).reshape(
        kv_heads, query_head_group, tok_rows, HEAD_SIZE
    )
    attention = (
        attention.transpose(2, 0, 1, 3)
        .reshape(tok_rows, kv_heads * query_head_group * HEAD_SIZE)
        .astype(jnp.bfloat16)
    )
    partial_value = jnp.dot(
        lax.all_gather(attention, "ctx", axis=0, tiled=True),
        out_weight,
        preferred_element_type=jnp.float32,
    ).astype(jnp.bfloat16)
    term_rows = lax.all_to_all(
        partial_value, "ctx", split_axis=0, concat_axis=1, tiled=True
    ).astype(jnp.float32)
    summed = lax.psum_scatter(
        term_rows.astype(jnp.bfloat16), "tp", scatter_dimension=1, tiled=True
    ).astype(jnp.float32)
    hidden_out = (residual.astype(jnp.float32) + summed).astype(jnp.bfloat16)
    token_score = jnp.dot(hidden_out, value_head, preferred_element_type=jnp.float32)
    one_hot = (turn_ids[:, None] == jnp.arange(TURNS, dtype=jnp.int32)[None, :]).astype(jnp.float32)
    local_sum = jnp.dot(token_score, one_hot, precision=lax.Precision.HIGHEST)
    local_count = jnp.where(lax.axis_index("tp") == 0, jnp.sum(one_hot, axis=0), 0.0)
    totals, counts = lax.psum((local_sum, local_count), ("ctx", "tp"))
    turn_means = totals / jnp.maximum(counts, 1.0)
    return (hidden_out, turn_means)


MESH = pl.DeviceIdType.MESH
F32 = jnp.float32
BF16 = jnp.bfloat16


def kernel(
    dims, q_ref, k_ref, v_ref, seg_ref, pos_ref, tid_ref, vh_ref, res_hbm, w_hbm,
    out_ref, mean_ref,
    kg, vg, cg, ccol, ids, tcol, qrow, qs, ot, att, wv, acc, part, rs, red, fin, resv, tot,
    k_send, v_send, c_send, k_recv, v_recv, c_recv, att_send, att_recv,
    rs_send, rs_recv, fin_send, fin_recv, tot_send, tot_recv, w_sem, res_sem,
):
    n, tn, rows, groups, per, cb, lanes = dims
    c = lax.axis_index("ctx")
    t = lax.axis_index("tp")
    keys_all = n * rows
    half = per * HEAD_SIZE
    scale = 1.0 / math.sqrt(HEAD_SIZE)

    barrier = pltpu.get_barrier_semaphore()

    def greet(i, _):
        other = lax.rem(c * tn + t + 1 + i, n * tn)
        pl.semaphore_signal(
            barrier, inc=1, device_id={"ctx": other // tn, "tp": lax.rem(other, tn)},
            device_id_type=MESH,
        )
        return 0

    lax.fori_loop(0, n * tn - 1, greet, 0)

    def w_copy(i):
        return pltpu.make_async_copy(
            w_hbm.at[:, pl.ds(pl.multiple_of(i * cb, 128), cb)], wv.at[i], w_sem.at[i]
        )

    res_copy = pltpu.make_async_copy(res_hbm, resv, res_sem)

    ids[...] = jnp.zeros_like(ids)
    low = seg_ref[...].reshape(1, rows) * keys_all
    ids[0:1, 0:rows] = low + pos_ref[...].reshape(1, rows)
    ids[1:2, 0:rows] = low
    ids[2:3, 0:rows] = tid_ref[...].reshape(1, rows)
    cg[c] = ids[0:8, :]
    for g in range(groups):
        kg[g, c] = k_ref[:, g * HEAD_SIZE:(g + 1) * HEAD_SIZE]
        vg[g, c] = v_ref[:, g * HEAD_SIZE:(g + 1) * HEAD_SIZE]
    pl.semaphore_wait(barrier, n * tn - 1)

    def kv_copies(g, src, dst, slot):
        dev = {"ctx": dst}
        span = slice(g * HEAD_SIZE, (g + 1) * HEAD_SIZE)
        plan = [
            (k_ref.at[:, span], kg.at[g, src], k_send.at[g, slot], k_recv.at[g, src]),
            (v_ref.at[:, span], vg.at[g, src], v_send.at[g, slot], v_recv.at[g, src]),
        ]
        if g == 0:
            plan.insert(0, (cg.at[src], cg.at[src], c_send.at[slot], c_recv.at[src]))
        return [
            pltpu.make_async_remote_copy(
                src_ref=a, dst_ref=b, send_sem=x, recv_sem=y, device_id=dev, device_id_type=MESH
            )
            for a, b, x, y in plan
        ]

    def att_copy(s, g, d):
        return pltpu.make_async_remote_copy(
            src_ref=att.at[s, g], dst_ref=att.at[s, g],
            send_sem=att_send.at[d, s, g], recv_sem=att_recv.at[s, g],
            device_id={"ctx": c + 1 - 2 * d}, device_id_type=MESH,
        )

    def rs_copy(s, i):
        return pltpu.make_async_remote_copy(
            src_ref=part.at[s, i], dst_ref=rs.at[s, t],
            send_sem=rs_send.at[s, i], recv_sem=rs_recv.at[s, t],
            device_id={"tp": i}, device_id_type=MESH,
        )

    def rs_arrival(s, i):
        return pltpu.make_async_remote_copy(
            src_ref=part.at[s, i], dst_ref=rs.at[s, i],
            send_sem=rs_send.at[s, i], recv_sem=rs_recv.at[s, i],
            device_id={"tp": i}, device_id_type=MESH,
        )

    def fin_copy(s):
        return pltpu.make_async_remote_copy(
            src_ref=red.at[s], dst_ref=fin.at[t],
            send_sem=fin_send.at[s], recv_sem=fin_recv.at[t],
            device_id={"ctx": s, "tp": c}, device_id_type=MESH,
        )

    def fin_arrival(i):
        return pltpu.make_async_remote_copy(
            src_ref=red.at[0], dst_ref=fin.at[i],
            send_sem=fin_send.at[0], recv_sem=fin_recv.at[i],
            device_id={"ctx": t, "tp": i}, device_id_type=MESH,
        )

    def goes(s, d):
        if d == 0:
            return (s <= c) & (c < n - 1)
        return (s >= c) & (c > 0)

    for g in range(groups):
        for j in range(1, n):
            dst = lax.rem(c + j, n)
            for cp in kv_copies(g, c, dst, dst):
                cp.start()
    for i in range(tn):
        w_copy(i).start()
    res_copy.start()

    for g in range(groups):
        for h in range(per):
            col = (g * per + h) * HEAD_SIZE
            qs[g, h * rows:(h + 1) * rows, :] = q_ref[:, col:col + HEAD_SIZE]
    idcol = ids[...].T[:rows, :]
    tcol[...] = idcol[:, 2:3]
    qrow[...] = jnp.concatenate([idcol] * per, axis=0).T[0:8, :]

    for g in range(groups):
        for j in range(1, n):
            src = lax.rem(c + n - j, n)
            for cp in kv_copies(g, src, src, src):
                cp.wait_recv()
        if g == 0:
            for s in range(n):
                ids[s:s + 1, :] = cg[s, 0:1, :]
            columns = ids[...].T[:rows, :]
            for s in range(n):
                ccol[s] = columns[:, s:s + 1]

        def score_step(i, _):
            span = pl.ds(pl.multiple_of(i * lanes, 128), lanes)
            keys = kg[g].reshape(keys_all, HEAD_SIZE)
            vals = vg[g].reshape(keys_all, HEAD_SIZE)
            s = lax.dot_general(
                keys, qs[g, span, :], (((1,), (1,)), ((), ())), preferred_element_type=F32
            ) * scale
            cj = ccol[...].reshape(keys_all, 1)
            allowed = (cj <= qrow[0:1, span]) & (cj >= qrow[1:2, span])
            s = jnp.where(allowed, s, -1e30)
            top = jnp.max(s, axis=0, keepdims=True)
            p = jnp.where(allowed, jnp.exp(s - top), 0.0)
            den = jnp.sum(p, axis=0, keepdims=True)
            o = lax.dot_general(
                vals, p.astype(BF16), (((0,), (0,)), ((), ())), preferred_element_type=F32
            )
            ot[span, :] = (o / den).T.astype(BF16)
            return 0

        lax.fori_loop(0, per * rows // lanes, score_step, 0)
        for h in range(per):
            att[c, g, :, h * HEAD_SIZE:(h + 1) * HEAD_SIZE] = ot[h * rows:(h + 1) * rows, :]
        for d in range(2):
            @pl.when(goes(c, d))
            def _():
                att_copy(c, g, d).start()

    for i in range(tn):
        w_copy(i).wait()

    def column_of(j):
        if tn == 4:
            odd = lax.rem(t, 2)
            shift = jnp.where(
                j == 0, 2, jnp.where(j == 1, 3 - 2 * odd, jnp.where(j == 2, 1 + 2 * odd, 0))
            )
            return lax.rem(t + shift, tn)
        return lax.rem(t + 1 + j, tn)

    def project(s, side, g):
        def column(j, _):
            i = column_of(j)
            prod = jnp.dot(
                att[s, g], wv[i, g * half:(g + 1) * half, :], preferred_element_type=F32
            )
            if g > 0:
                prod = acc[side, i] + prod
            if g < groups - 1:
                acc[side, i] = prod
                return 0
            value = prod.astype(BF16)

            @pl.when(i == t)
            def _():
                rs[s, t] = value

            @pl.when(i != t)
            def _():
                part[s, i] = value
                rs_copy(s, i).start()

            return 0

        lax.fori_loop(0, tn, column, 0)

    def reduce_send(s):
        for i in range(tn):
            @pl.when(t != i)
            def _():
                rs_arrival(s, i).wait_recv()
        total = None
        for i in range(tn):
            term = rs[s, i].astype(F32)
            total = term if total is None else total + term
        summed = total.astype(BF16)
        mine = (s == c) & (t == c)

        @pl.when(mine)
        def _():
            fin[t] = summed

        @pl.when(jnp.logical_not(mine))
        def _():
            red[s] = summed
            fin_copy(s).start()

    def both_sides(k, act):
        def one(side, _):
            s = c + k * (2 * side - 1)

            @pl.when((s >= 0) & (s < n) & ((k > 0) | (side == 0)))
            def _():
                act(s, side)

            return 0

        lax.fori_loop(0, 2, one, 0)

    for g in range(groups):
        project(c, 0, g)

    def step(k, _):
        for g in range(groups):
            def take(s, side):
                att_copy(s, g, 0).wait_recv()
                for d in range(2):
                    @pl.when(goes(s, d))
                    def _():
                        att_copy(s, g, d).start()

            both_sides(k, take)
            both_sides(k, lambda s, side: project(s, side, g))
            if g == 0:
                both_sides(k - 1, lambda s, side: reduce_send(s))
        return 0

    lax.fori_loop(1, n, step, 0)
    both_sides(n - 1, lambda s, side: reduce_send(s))

    res_copy.wait()
    score = jnp.zeros((rows, 1), F32)
    for i in range(tn):
        @pl.when(jnp.logical_not((c == t) & (t == i)))
        def _():
            fin_arrival(i).wait_recv()
        span = slice(i * cb, (i + 1) * cb)
        hidden = (resv[:, span].astype(F32) + fin[i].astype(F32)).astype(BF16)
        out_ref[:, span] = hidden
        score = score + jnp.sum(
            hidden.astype(F32) * vh_ref[span].astype(F32).reshape(1, cb), axis=1, keepdims=True
        )
    turn = lax.broadcasted_iota(jnp.int32, (rows, 128), 1)
    hot = (tcol[...] == turn).astype(F32)
    sums = jnp.sum(hot * score, axis=0, keepdims=True)
    counts = jnp.sum(hot, axis=0, keepdims=True)
    counts = counts * jnp.where(t == 0, 1.0, 0.0)
    row = lax.broadcasted_iota(jnp.int32, (8, 128), 0)
    me = c * tn + t
    tot[me] = jnp.where(row == 0, sums, jnp.where(row == 1, counts, 0.0))

    def tot_copy(j):
        other = lax.rem(me + j, n * tn)
        return pltpu.make_async_remote_copy(
            src_ref=tot.at[me], dst_ref=tot.at[me],
            send_sem=tot_send.at[other], recv_sem=tot_recv.at[me],
            device_id={"ctx": other // tn, "tp": lax.rem(other, tn)}, device_id_type=MESH,
        )

    def tot_arrival(j):
        other = lax.rem(me + j, n * tn)
        return pltpu.make_async_remote_copy(
            src_ref=tot.at[me], dst_ref=tot.at[other],
            send_sem=tot_send.at[other], recv_sem=tot_recv.at[other],
            device_id={"ctx": other // tn, "tp": lax.rem(other, tn)}, device_id_type=MESH,
        )

    def tot_start(j, _):
        tot_copy(j).start()
        return 0

    lax.fori_loop(1, n * tn, tot_start, 0)

    def drain(s, _):
        @pl.when(s != c)
        def _():
            for g in range(groups):
                for cp in kv_copies(g, c, s, s):
                    cp.wait_send()

        for d in range(2):
            @pl.when(goes(s, d))
            def _():
                for g in range(groups):
                    att_copy(s, g, d).wait_send()
        for i in range(tn):
            @pl.when(t != i)
            def _():
                rs_copy(s, i).wait_send()

        @pl.when(jnp.logical_not((s == c) & (t == c)))
        def _():
            fin_copy(s).wait_send()

        return 0

    lax.fori_loop(0, n, drain, 0)

    def tot_wait(j, _):
        tot_arrival(j).wait_recv()
        tot_copy(j).wait_send()
        return 0

    lax.fori_loop(1, n * tn, tot_wait, 0)
    whole = jnp.sum(tot[...], axis=0)
    mean_ref[...] = whole[0:1, :TURNS] / jnp.maximum(whole[1:2, :TURNS], 1.0)


def fused(
    n, tn, queries, keys, values, residual, out_weight, value_head, segment_ids, positions, turn_ids
):
    rows, width = queries.shape
    groups = keys.shape[1] // HEAD_SIZE
    per = width // keys.shape[1]
    cols = out_weight.shape[1]
    cb = cols // tn
    lanes = next(x for x in (384, 256, 128) if (per * rows) % x == 0)
    padded = -(-rows // 128) * 128
    dims = (n, tn, rows, groups, per, cb, lanes)
    vmem = pl.BlockSpec(memory_space=pltpu.VMEM)
    hbm = pl.BlockSpec(memory_space=pl.ANY)
    dma = pltpu.SemaphoreType.DMA
    out, means = pl.pallas_call(
        functools.partial(kernel, dims),
        out_shape=(
            jax.ShapeDtypeStruct((rows, cols), BF16),
            jax.ShapeDtypeStruct((1, TURNS), F32),
        ),
        in_specs=[vmem] * 7 + [hbm] * 2,
        out_specs=(vmem, vmem),
        scratch_shapes=[
            pltpu.VMEM((groups, n, rows, HEAD_SIZE), BF16),
            pltpu.VMEM((groups, n, rows, HEAD_SIZE), BF16),
            pltpu.VMEM((n, 8, padded), jnp.int32),
            pltpu.VMEM((n, rows, 1), jnp.int32),
            pltpu.VMEM((128, padded), jnp.int32),
            pltpu.VMEM((rows, 1), jnp.int32),
            pltpu.VMEM((8, per * rows), jnp.int32),
            pltpu.VMEM((groups, per * rows, HEAD_SIZE), BF16),
            pltpu.VMEM((per * rows, HEAD_SIZE), BF16),
            pltpu.VMEM((n, groups, rows, per * HEAD_SIZE), BF16),
            pltpu.VMEM((tn, width, cb), BF16),
            pltpu.VMEM((2, tn, rows, cb), F32),
            pltpu.VMEM((n, tn, rows, cb), BF16),
            pltpu.VMEM((n, tn, rows, cb), BF16),
            pltpu.VMEM((n, rows, cb), BF16),
            pltpu.VMEM((tn, rows, cb), BF16),
            pltpu.VMEM((rows, cols), BF16),
            pltpu.VMEM((n * tn, 8, 128), F32),
            dma((groups, n)), dma((groups, n)), dma((n,)),
            dma((groups, n)), dma((groups, n)), dma((n,)),
            dma((2, n, groups)), dma((n, groups)),
            dma((n, tn)), dma((n, tn)),
            dma((n,)), dma((tn,)),
            dma((n * tn,)), dma((n * tn,)),
            dma((tn,)), dma(()),
        ],
        compiler_params=pltpu.CompilerParams(
            collective_id=0, has_side_effects=True, vmem_limit_bytes=56 * 1024 * 1024
        ),
    )(
        queries, keys, values, segment_ids, positions, turn_ids,
        value_head, residual, out_weight,
    )
    return out, means.reshape(TURNS)


def body(n, tn, *args):
    queries, weight = args[0], args[4]
    rows = queries.shape[0]
    fits = n == tn and n <= 128 and rows % 16 == 0 and weight.shape[1] % (128 * tn) == 0
    if fits:
        return fused(n, tn, *args)
    return shards(*args)


def solution(mesh):
    return jax.shard_map(
        functools.partial(body, mesh.shape["ctx"], mesh.shape["tp"]),
        mesh=mesh,
        in_specs=(
            P(("groups", "ctx"), "tp"),
            P(("groups", "ctx"), "tp"),
            P(("groups", "ctx"), "tp"),
            P(("groups", "ctx"), "tp"),
            P("tp", "ctx"),
            P("tp"),
            P(("groups", "ctx")),
            P(("groups", "ctx")),
            P(("groups", "ctx")),
        ),
        out_specs=(P(("groups", "ctx"), "tp"), P("groups")),
        check_vma=False,
    )
```

```python
import functools
import math

import jax
import jax.numpy as jnp
from jax import lax
from jax.experimental import pallas as pl
from jax.experimental.pallas import tpu as pltpu
from jax.sharding import PartitionSpec as P

HEAD_SIZE = 128
TURNS = 16


def shards(
    queries, keys, values, residual, out_weight, value_head, segment_ids, positions, turn_ids
):
    tok_rows = queries.shape[0]
    kv_heads = keys.shape[1] // HEAD_SIZE
    query_head_group = queries.shape[1] // keys.shape[1]
    query_rows = query_head_group * tok_rows
    score_scale = 1.0 / math.sqrt(HEAD_SIZE)
    grouped = (
        queries.reshape(tok_rows, kv_heads, query_head_group, HEAD_SIZE)
        .transpose(1, 2, 0, 3)
        .reshape(kv_heads, query_rows, HEAD_SIZE)
    )
    seg_rows = jnp.tile(segment_ids, query_head_group)
    pos_rows = jnp.tile(positions, query_head_group)

    def update(running, key_block, value_block, seg_block, pos_block):
        allowed = (seg_rows[:, None] == seg_block[None, :]) & (
            pos_block[None, :] <= pos_rows[:, None]
        )
        numerator, row_max, denominator = running
        scores = (
            jnp.einsum("hqd,khd->hqk", grouped, key_block, preferred_element_type=jnp.float32)
            * score_scale
        )
        scores = jnp.where(allowed[None], scores, -1e30)
        new_max = jnp.maximum(row_max, jnp.max(scores, axis=2))
        weights = jnp.where(allowed[None], jnp.exp(scores - new_max[..., None]), 0.0)
        factor = jnp.exp(row_max - new_max)
        denominator = denominator * factor + jnp.sum(weights, axis=2)
        product = jnp.einsum(
            "hqk,khd->hqd",
            weights.astype(jnp.bfloat16),
            value_block,
            preferred_element_type=jnp.float32,
        )
        numerator = numerator * factor[..., None] + product
        return (numerator, new_max, denominator)

    initial = (
        jnp.zeros((kv_heads, query_rows, HEAD_SIZE), jnp.float32),
        jnp.full((kv_heads, query_rows), -1e30, jnp.float32),
        jnp.zeros((kv_heads, query_rows), jnp.float32),
    )
    running = initial
    key_piece = lax.all_gather(keys, "ctx", axis=0, tiled=True)
    value_piece = lax.all_gather(values, "ctx", axis=0, tiled=True)
    seg_piece = lax.all_gather(segment_ids, "ctx", axis=0, tiled=True)
    pos_piece = lax.all_gather(positions, "ctx", axis=0, tiled=True)
    row_count = key_piece.shape[0]
    key_piece = key_piece.reshape(row_count, kv_heads, HEAD_SIZE)
    value_piece = value_piece.reshape(row_count, kv_heads, HEAD_SIZE)
    block_width = math.gcd(row_count, 512)
    block_steps = row_count // block_width
    stacked = (
        key_piece.reshape(block_steps, block_width, kv_heads, HEAD_SIZE),
        value_piece.reshape(block_steps, block_width, kv_heads, HEAD_SIZE),
        seg_piece.reshape(block_steps, block_width),
        pos_piece.reshape(block_steps, block_width),
    )

    def block_step(running_state, block_set):
        return (update(running_state, block_set[0], block_set[1], block_set[2], block_set[3]), None)

    running, _ = lax.scan(block_step, running, stacked)
    numerator, row_max, denominator = running
    attention = (numerator / denominator[..., None]).reshape(
        kv_heads, query_head_group, tok_rows, HEAD_SIZE
    )
    attention = (
        attention.transpose(2, 0, 1, 3)
        .reshape(tok_rows, kv_heads * query_head_group * HEAD_SIZE)
        .astype(jnp.bfloat16)
    )
    partial_value = jnp.dot(
        lax.all_gather(attention, "ctx", axis=0, tiled=True),
        out_weight,
        preferred_element_type=jnp.float32,
    ).astype(jnp.bfloat16)
    term_rows = lax.all_to_all(
        partial_value, "ctx", split_axis=0, concat_axis=1, tiled=True
    ).astype(jnp.float32)
    summed = lax.psum_scatter(
        term_rows.astype(jnp.bfloat16), "tp", scatter_dimension=1, tiled=True
    ).astype(jnp.float32)
    hidden_out = (residual.astype(jnp.float32) + summed).astype(jnp.bfloat16)
    token_score = jnp.dot(hidden_out, value_head, preferred_element_type=jnp.float32)
    one_hot = (turn_ids[:, None] == jnp.arange(TURNS, dtype=jnp.int32)[None, :]).astype(jnp.float32)
    local_sum = jnp.dot(token_score, one_hot, precision=lax.Precision.HIGHEST)
    local_count = jnp.where(lax.axis_index("tp") == 0, jnp.sum(one_hot, axis=0), 0.0)
    totals, counts = lax.psum((local_sum, local_count), ("ctx", "tp"))
    turn_means = totals / jnp.maximum(counts, 1.0)
    return (hidden_out, turn_means)


MESH = pl.DeviceIdType.MESH
F32 = jnp.float32
BF16 = jnp.bfloat16


def kernel(
    dims, q_ref, k_ref, v_ref, seg_ref, pos_ref, tid_ref, vh_ref, res_hbm, w_hbm,
    out_ref, mean_ref,
    kg, vg, cg, ccol, ids, tcol, qrow, qs, ot, att, wv, acc, part, rs, red, fin, resv, tot,
    k_send, v_send, c_send, k_recv, v_recv, c_recv, att_send, att_recv,
    rs_send, rs_recv, fin_send, fin_recv, tot_send, tot_recv, w_sem, res_sem,
):
    n, tn, rows, groups, per, cb, lanes, pieces = dims
    piece = rows // pieces
    c = lax.axis_index("ctx")
    t = lax.axis_index("tp")
    keys_all = n * rows
    half = per * HEAD_SIZE
    scale = 1.0 / math.sqrt(HEAD_SIZE)

    barrier = pltpu.get_barrier_semaphore()

    def greet(i, _):
        other = lax.rem(c * tn + t + 1 + i, n * tn)
        pl.semaphore_signal(
            barrier, inc=1, device_id={"ctx": other // tn, "tp": lax.rem(other, tn)},
            device_id_type=MESH,
        )
        return 0

    lax.fori_loop(0, n * tn - 1, greet, 0)

    def w_copy(i):
        return pltpu.make_async_copy(
            w_hbm.at[:, pl.ds(pl.multiple_of(i * cb, 128), cb)], wv.at[i], w_sem.at[i]
        )

    res_copy = pltpu.make_async_copy(res_hbm, resv, res_sem)

    ids[...] = jnp.zeros_like(ids)
    low = seg_ref[...].reshape(1, rows) * keys_all
    ids[0:1, 0:rows] = low + pos_ref[...].reshape(1, rows)
    ids[1:2, 0:rows] = low
    ids[2:3, 0:rows] = tid_ref[...].reshape(1, rows)
    cg[c] = ids[0:8, :]
    for g in range(groups):
        kg[g, c] = k_ref[:, g * HEAD_SIZE:(g + 1) * HEAD_SIZE]
        vg[g, c] = v_ref[:, g * HEAD_SIZE:(g + 1) * HEAD_SIZE]
    pl.semaphore_wait(barrier, n * tn - 1)

    def kv_copies(g, src, dst, slot):
        dev = {"ctx": dst}
        span = slice(g * HEAD_SIZE, (g + 1) * HEAD_SIZE)
        plan = [
            (k_ref.at[:, span], kg.at[g, src], k_send.at[g, slot], k_recv.at[g, src]),
            (v_ref.at[:, span], vg.at[g, src], v_send.at[g, slot], v_recv.at[g, src]),
        ]
        if g == 0:
            plan.insert(0, (cg.at[src], cg.at[src], c_send.at[slot], c_recv.at[src]))
        return [
            pltpu.make_async_remote_copy(
                src_ref=a, dst_ref=b, send_sem=x, recv_sem=y, device_id=dev, device_id_type=MESH
            )
            for a, b, x, y in plan
        ]

    def att_copy(s, g, d):
        return pltpu.make_async_remote_copy(
            src_ref=att.at[s, g], dst_ref=att.at[s, g],
            send_sem=att_send.at[d, s, g], recv_sem=att_recv.at[s, g],
            device_id={"ctx": c + 1 - 2 * d}, device_id_type=MESH,
        )

    def band(p):
        return pl.ds(p * piece, piece)

    def rs_copy(s, i, p):
        return pltpu.make_async_remote_copy(
            src_ref=part.at[s, i, band(p)], dst_ref=rs.at[s, t, band(p)],
            send_sem=rs_send.at[s, i, p], recv_sem=rs_recv.at[s, t, p],
            device_id={"tp": i}, device_id_type=MESH,
        )

    def rs_arrival(s, i, p):
        return pltpu.make_async_remote_copy(
            src_ref=part.at[s, i, band(p)], dst_ref=rs.at[s, i, band(p)],
            send_sem=rs_send.at[s, i, p], recv_sem=rs_recv.at[s, i, p],
            device_id={"tp": i}, device_id_type=MESH,
        )

    def fin_copy(s, p):
        return pltpu.make_async_remote_copy(
            src_ref=red.at[s, band(p)], dst_ref=fin.at[t, band(p)],
            send_sem=fin_send.at[s, p], recv_sem=fin_recv.at[t, p],
            device_id={"ctx": s, "tp": c}, device_id_type=MESH,
        )

    def fin_arrival(i, p):
        return pltpu.make_async_remote_copy(
            src_ref=red.at[0, band(p)], dst_ref=fin.at[i, band(p)],
            send_sem=fin_send.at[0, p], recv_sem=fin_recv.at[i, p],
            device_id={"ctx": t, "tp": i}, device_id_type=MESH,
        )

    def goes(s, d):
        if d == 0:
            return (s <= c) & (c < n - 1)
        return (s >= c) & (c > 0)

    for g in range(groups):
        for j in range(1, n):
            dst = lax.rem(c + j, n)
            for cp in kv_copies(g, c, dst, dst):
                cp.start()
    for i in range(tn):
        w_copy(i).start()
    res_copy.start()

    for g in range(groups):
        for h in range(per):
            col = (g * per + h) * HEAD_SIZE
            qs[g, h * rows:(h + 1) * rows, :] = q_ref[:, col:col + HEAD_SIZE]
    idcol = ids[...].T[:rows, :]
    tcol[...] = idcol[:, 2:3]
    qrow[...] = jnp.concatenate([idcol] * per, axis=0).T[0:8, :]

    for g in range(groups):
        for j in range(1, n):
            src = lax.rem(c + n - j, n)
            for cp in kv_copies(g, src, src, src):
                cp.wait_recv()
        if g == 0:
            for s in range(n):
                ids[s:s + 1, :] = cg[s, 0:1, :]
            columns = ids[...].T[:rows, :]
            for s in range(n):
                ccol[s] = columns[:, s:s + 1]

        def score_step(i, _):
            span = pl.ds(pl.multiple_of(i * lanes, 128), lanes)
            keys = kg[g].reshape(keys_all, HEAD_SIZE)
            vals = vg[g].reshape(keys_all, HEAD_SIZE)
            s = lax.dot_general(
                keys, qs[g, span, :], (((1,), (1,)), ((), ())), preferred_element_type=F32
            ) * scale
            cj = ccol[...].reshape(keys_all, 1)
            allowed = (cj <= qrow[0:1, span]) & (cj >= qrow[1:2, span])
            s = jnp.where(allowed, s, -1e30)
            top = jnp.max(s, axis=0, keepdims=True)
            p = jnp.where(allowed, jnp.exp(s - top), 0.0)
            den = jnp.sum(p, axis=0, keepdims=True)
            o = lax.dot_general(
                vals, p.astype(BF16), (((0,), (0,)), ((), ())), preferred_element_type=F32
            )
            ot[span, :] = (o / den).T.astype(BF16)
            return 0

        lax.fori_loop(0, per * rows // lanes, score_step, 0)
        for h in range(per):
            att[c, g, :, h * HEAD_SIZE:(h + 1) * HEAD_SIZE] = ot[h * rows:(h + 1) * rows, :]
        for d in range(2):
            @pl.when(goes(c, d))
            def _():
                att_copy(c, g, d).start()

    for i in range(tn):
        w_copy(i).wait()

    def column_of(j):
        if tn == 4:
            odd = lax.rem(t, 2)
            shift = jnp.where(
                j == 0, 2, jnp.where(j == 1, 3 - 2 * odd, jnp.where(j == 2, 1 + 2 * odd, 0))
            )
            return lax.rem(t + shift, tn)
        return lax.rem(t + 1 + j, tn)

    def project(s, side, g):
        def column(j, _):
            i = column_of(j)
            prod = jnp.dot(
                att[s, g], wv[i, g * half:(g + 1) * half, :], preferred_element_type=F32
            )
            if g > 0:
                prod = acc[side, i] + prod
            if g < groups - 1:
                acc[side, i] = prod
                return 0
            value = prod.astype(BF16)

            @pl.when(i == t)
            def _():
                rs[s, t] = value

            @pl.when(i != t)
            def _():
                part[s, i] = value

            if tn == 4:
                @pl.when(j == 1)
                def _():
                    for p in range(pieces):
                        rs_copy(s, column_of(0), p).start()
                        rs_copy(s, i, p).start()

                @pl.when(j == 2)
                def _():
                    for p in range(pieces):
                        rs_copy(s, i, p).start()
            else:
                @pl.when(i != t)
                def _():
                    for p in range(pieces):
                        rs_copy(s, i, p).start()

            return 0

        lax.fori_loop(0, tn, column, 0)

    def reduce_send(s):
        mine = (s == c) & (t == c)
        for p in range(pieces):
            for i in range(tn):
                @pl.when(t != i)
                def _():
                    rs_arrival(s, i, p).wait_recv()
            rng = slice(p * piece, (p + 1) * piece)
            total = None
            for i in range(tn):
                term = rs[s, i, rng, :].astype(F32)
                total = term if total is None else total + term
            summed = total.astype(BF16)

            @pl.when(mine)
            def _():
                fin[t, rng, :] = summed

            @pl.when(jnp.logical_not(mine))
            def _():
                red[s, rng, :] = summed
                fin_copy(s, p).start()

    def both_sides(k, act):
        def one(side, _):
            s = c + k * (2 * side - 1)

            @pl.when((s >= 0) & (s < n) & ((k > 0) | (side == 0)))
            def _():
                act(s, side)

            return 0

        lax.fori_loop(0, 2, one, 0)

    for g in range(groups):
        project(c, 0, g)

    def step(k, _):
        for g in range(groups):
            def take(s, side):
                att_copy(s, g, 0).wait_recv()
                for d in range(2):
                    @pl.when(goes(s, d))
                    def _():
                        att_copy(s, g, d).start()

            both_sides(k, take)
            both_sides(k, lambda s, side: project(s, side, g))
            if g == 0:
                both_sides(k - 1, lambda s, side: reduce_send(s))
        return 0

    lax.fori_loop(1, n, step, 0)
    both_sides(n - 1, lambda s, side: reduce_send(s))

    res_copy.wait()
    line = jnp.zeros((1, 128), F32)
    lane = lax.broadcasted_iota(jnp.int32, (piece, 128), 1)
    one = jnp.where(t == 0, 1.0, 0.0)
    for p in range(pieces):
        rng = slice(p * piece, (p + 1) * piece)
        score = jnp.zeros((piece, 1), F32)
        for i in range(tn):
            @pl.when(jnp.logical_not((c == t) & (t == i)))
            def _():
                fin_arrival(i, p).wait_recv()
            span = slice(i * cb, (i + 1) * cb)
            hidden = (resv[rng, span].astype(F32) + fin[i, rng, :].astype(F32)).astype(BF16)
            out_ref[rng, span] = hidden
            score = score + jnp.sum(
                hidden.astype(F32) * vh_ref[span].astype(F32).reshape(1, cb), axis=1, keepdims=True
            )
        turn = tcol[rng, :]
        terms = jnp.where(turn == lane, score, jnp.where(turn + 64 == lane, one, 0.0))
        line = line + jnp.sum(terms, axis=0, keepdims=True)
    me = c * tn + t
    tot[me] = line

    def tot_copy(j):
        other = lax.rem(me + j, n * tn)
        return pltpu.make_async_remote_copy(
            src_ref=tot.at[me], dst_ref=tot.at[me],
            send_sem=tot_send.at[other], recv_sem=tot_recv.at[me],
            device_id={"ctx": other // tn, "tp": lax.rem(other, tn)}, device_id_type=MESH,
        )

    def tot_arrival(j):
        other = lax.rem(me + j, n * tn)
        return pltpu.make_async_remote_copy(
            src_ref=tot.at[me], dst_ref=tot.at[other],
            send_sem=tot_send.at[other], recv_sem=tot_recv.at[other],
            device_id={"ctx": other // tn, "tp": lax.rem(other, tn)}, device_id_type=MESH,
        )

    def tot_start(j, _):
        tot_copy(j).start()
        return 0

    lax.fori_loop(1, n * tn, tot_start, 0)

    def drain(s, _):
        @pl.when(s != c)
        def _():
            for g in range(groups):
                for cp in kv_copies(g, c, s, s):
                    cp.wait_send()

        for d in range(2):
            @pl.when(goes(s, d))
            def _():
                for g in range(groups):
                    att_copy(s, g, d).wait_send()
        for i in range(tn):
            @pl.when(t != i)
            def _():
                for p in range(pieces):
                    rs_copy(s, i, p).wait_send()

        @pl.when(jnp.logical_not((s == c) & (t == c)))
        def _():
            for p in range(pieces):
                fin_copy(s, p).wait_send()

        return 0

    lax.fori_loop(0, n, drain, 0)

    def tot_wait(j, _):
        tot_arrival(j).wait_recv()
        tot_copy(j).wait_send()
        return 0

    lax.fori_loop(1, n * tn, tot_wait, 0)
    mean_ref[...] = jnp.sum(tot[...], axis=0)


def fused(
    n, tn, queries, keys, values, residual, out_weight, value_head, segment_ids, positions, turn_ids
):
    rows, width = queries.shape
    groups = keys.shape[1] // HEAD_SIZE
    per = width // keys.shape[1]
    cols = out_weight.shape[1]
    cb = cols // tn
    lanes = next(x for x in (384, 256, 128) if (per * rows) % x == 0)
    padded = -(-rows // 128) * 128
    pieces = 3 if rows % 48 == 0 else 1
    dims = (n, tn, rows, groups, per, cb, lanes, pieces)
    vmem = pl.BlockSpec(memory_space=pltpu.VMEM)
    hbm = pl.BlockSpec(memory_space=pl.ANY)
    dma = pltpu.SemaphoreType.DMA
    out, means = pl.pallas_call(
        functools.partial(kernel, dims),
        out_shape=(
            jax.ShapeDtypeStruct((rows, cols), BF16),
            jax.ShapeDtypeStruct((1, 128), F32),
        ),
        in_specs=[vmem] * 7 + [hbm] * 2,
        out_specs=(vmem, vmem),
        scratch_shapes=[
            pltpu.VMEM((groups, n, rows, HEAD_SIZE), BF16),
            pltpu.VMEM((groups, n, rows, HEAD_SIZE), BF16),
            pltpu.VMEM((n, 8, padded), jnp.int32),
            pltpu.VMEM((n, rows, 1), jnp.int32),
            pltpu.VMEM((128, padded), jnp.int32),
            pltpu.VMEM((rows, 1), jnp.int32),
            pltpu.VMEM((8, per * rows), jnp.int32),
            pltpu.VMEM((groups, per * rows, HEAD_SIZE), BF16),
            pltpu.VMEM((per * rows, HEAD_SIZE), BF16),
            pltpu.VMEM((n, groups, rows, per * HEAD_SIZE), BF16),
            pltpu.VMEM((tn, width, cb), BF16),
            pltpu.VMEM((2, tn, rows, cb), F32),
            pltpu.VMEM((n, tn, rows, cb), BF16),
            pltpu.VMEM((n, tn, rows, cb), BF16),
            pltpu.VMEM((n, rows, cb), BF16),
            pltpu.VMEM((tn, rows, cb), BF16),
            pltpu.VMEM((rows, cols), BF16),
            pltpu.VMEM((n * tn, 1, 128), F32),
            dma((groups, n)), dma((groups, n)), dma((n,)),
            dma((groups, n)), dma((groups, n)), dma((n,)),
            dma((2, n, groups)), dma((n, groups)),
            dma((n, tn, pieces)), dma((n, tn, pieces)),
            dma((n, pieces)), dma((tn, pieces)),
            dma((n * tn,)), dma((n * tn,)),
            dma((tn,)), dma(()),
        ],
        compiler_params=pltpu.CompilerParams(
            collective_id=0, has_side_effects=True, vmem_limit_bytes=56 * 1024 * 1024
        ),
    )(
        queries, keys, values, segment_ids, positions, turn_ids,
        value_head, residual, out_weight,
    )
    return out, means[0, :TURNS] / jnp.maximum(means[0, 64:64 + TURNS], 1.0)


def body(n, tn, *args):
    queries, weight = args[0], args[4]
    rows = queries.shape[0]
    fits = n == tn and n <= 128 and rows % 16 == 0 and weight.shape[1] % (128 * tn) == 0
    if fits:
        return fused(n, tn, *args)
    return shards(*args)


def solution(mesh):
    return jax.shard_map(
        functools.partial(body, mesh.shape["ctx"], mesh.shape["tp"]),
        mesh=mesh,
        in_specs=(
            P(("groups", "ctx"), "tp"),
            P(("groups", "ctx"), "tp"),
            P(("groups", "ctx"), "tp"),
            P(("groups", "ctx"), "tp"),
            P("tp", "ctx"),
            P("tp"),
            P(("groups", "ctx")),
            P(("groups", "ctx")),
            P(("groups", "ctx")),
        ),
        out_specs=(P(("groups", "ctx"), "tp"), P("groups")),
        check_vma=False,
    )
```

```python
import functools
import math

import jax
import jax.numpy as jnp
from jax import lax
from jax.experimental import pallas as pl
from jax.experimental.pallas import tpu as pltpu
from jax.sharding import PartitionSpec as P

HEAD_SIZE = 128
TURNS = 16


def shards(
    queries, keys, values, residual, out_weight, value_head, segment_ids, positions, turn_ids
):
    tok_rows = queries.shape[0]
    kv_heads = keys.shape[1] // HEAD_SIZE
    query_head_group = queries.shape[1] // keys.shape[1]
    query_rows = query_head_group * tok_rows
    score_scale = 1.0 / math.sqrt(HEAD_SIZE)
    grouped = (
        queries.reshape(tok_rows, kv_heads, query_head_group, HEAD_SIZE)
        .transpose(1, 2, 0, 3)
        .reshape(kv_heads, query_rows, HEAD_SIZE)
    )
    seg_rows = jnp.tile(segment_ids, query_head_group)
    pos_rows = jnp.tile(positions, query_head_group)

    def update(running, key_block, value_block, seg_block, pos_block):
        allowed = (seg_rows[:, None] == seg_block[None, :]) & (
            pos_block[None, :] <= pos_rows[:, None]
        )
        numerator, row_max, denominator = running
        scores = (
            jnp.einsum("hqd,khd->hqk", grouped, key_block, preferred_element_type=jnp.float32)
            * score_scale
        )
        scores = jnp.where(allowed[None], scores, -1e30)
        new_max = jnp.maximum(row_max, jnp.max(scores, axis=2))
        weights = jnp.where(allowed[None], jnp.exp(scores - new_max[..., None]), 0.0)
        factor = jnp.exp(row_max - new_max)
        denominator = denominator * factor + jnp.sum(weights, axis=2)
        product = jnp.einsum(
            "hqk,khd->hqd",
            weights.astype(jnp.bfloat16),
            value_block,
            preferred_element_type=jnp.float32,
        )
        numerator = numerator * factor[..., None] + product
        return (numerator, new_max, denominator)

    initial = (
        jnp.zeros((kv_heads, query_rows, HEAD_SIZE), jnp.float32),
        jnp.full((kv_heads, query_rows), -1e30, jnp.float32),
        jnp.zeros((kv_heads, query_rows), jnp.float32),
    )
    running = initial
    key_piece = lax.all_gather(keys, "ctx", axis=0, tiled=True)
    value_piece = lax.all_gather(values, "ctx", axis=0, tiled=True)
    seg_piece = lax.all_gather(segment_ids, "ctx", axis=0, tiled=True)
    pos_piece = lax.all_gather(positions, "ctx", axis=0, tiled=True)
    row_count = key_piece.shape[0]
    key_piece = key_piece.reshape(row_count, kv_heads, HEAD_SIZE)
    value_piece = value_piece.reshape(row_count, kv_heads, HEAD_SIZE)
    block_width = math.gcd(row_count, 512)
    block_steps = row_count // block_width
    stacked = (
        key_piece.reshape(block_steps, block_width, kv_heads, HEAD_SIZE),
        value_piece.reshape(block_steps, block_width, kv_heads, HEAD_SIZE),
        seg_piece.reshape(block_steps, block_width),
        pos_piece.reshape(block_steps, block_width),
    )

    def block_step(running_state, block_set):
        return (update(running_state, block_set[0], block_set[1], block_set[2], block_set[3]), None)

    running, _ = lax.scan(block_step, running, stacked)
    numerator, row_max, denominator = running
    attention = (numerator / denominator[..., None]).reshape(
        kv_heads, query_head_group, tok_rows, HEAD_SIZE
    )
    attention = (
        attention.transpose(2, 0, 1, 3)
        .reshape(tok_rows, kv_heads * query_head_group * HEAD_SIZE)
        .astype(jnp.bfloat16)
    )
    partial_value = jnp.dot(
        lax.all_gather(attention, "ctx", axis=0, tiled=True),
        out_weight,
        preferred_element_type=jnp.float32,
    ).astype(jnp.bfloat16)
    term_rows = lax.all_to_all(
        partial_value, "ctx", split_axis=0, concat_axis=1, tiled=True
    ).astype(jnp.float32)
    summed = lax.psum_scatter(
        term_rows.astype(jnp.bfloat16), "tp", scatter_dimension=1, tiled=True
    ).astype(jnp.float32)
    hidden_out = (residual.astype(jnp.float32) + summed).astype(jnp.bfloat16)
    token_score = jnp.dot(hidden_out, value_head, preferred_element_type=jnp.float32)
    one_hot = (turn_ids[:, None] == jnp.arange(TURNS, dtype=jnp.int32)[None, :]).astype(jnp.float32)
    local_sum = jnp.dot(token_score, one_hot, precision=lax.Precision.HIGHEST)
    local_count = jnp.where(lax.axis_index("tp") == 0, jnp.sum(one_hot, axis=0), 0.0)
    totals, counts = lax.psum((local_sum, local_count), ("ctx", "tp"))
    turn_means = totals / jnp.maximum(counts, 1.0)
    return (hidden_out, turn_means)


MESH = pl.DeviceIdType.MESH
F32 = jnp.float32
BF16 = jnp.bfloat16


def kernel(
    dims, q_ref, k_ref, v_ref, seg_ref, pos_ref, tid_ref, vh_ref, res_hbm, w_hbm,
    out_ref, mean_ref,
    kg, vg, cg, ccol, ids, tcol, qrow, qs, ot, att, wv, acc, part, rs, red, fin, resv, tot,
    k_send, v_send, c_send, k_recv, v_recv, c_recv, att_send, att_recv,
    rs_send, rs_recv, fin_send, fin_recv, tot_send, tot_recv, w_sem, res_sem,
):
    n, tn, rows, groups, per, cb, lanes, pieces = dims
    piece = rows // pieces
    c = lax.axis_index("ctx")
    t = lax.axis_index("tp")
    keys_all = n * rows
    half = per * HEAD_SIZE
    scale = 1.0 / math.sqrt(HEAD_SIZE)

    barrier = pltpu.get_barrier_semaphore()

    def greet(i, _):
        other = lax.rem(c * tn + t + 1 + i, n * tn)
        pl.semaphore_signal(
            barrier, inc=1, device_id={"ctx": other // tn, "tp": lax.rem(other, tn)},
            device_id_type=MESH,
        )
        return 0

    lax.fori_loop(0, n * tn - 1, greet, 0)

    def w_copy(i):
        return pltpu.make_async_copy(
            w_hbm.at[:, pl.ds(pl.multiple_of(i * cb, 128), cb)], wv.at[i], w_sem.at[i]
        )

    res_copy = pltpu.make_async_copy(res_hbm, resv, res_sem)

    ids[...] = jnp.zeros_like(ids)
    low = seg_ref[...].reshape(1, rows) * keys_all
    ids[0:1, 0:rows] = low + pos_ref[...].reshape(1, rows)
    ids[1:2, 0:rows] = low
    ids[2:3, 0:rows] = tid_ref[...].reshape(1, rows)
    cg[c] = ids[0:8, :]
    for g in range(groups):
        kg[g, c] = k_ref[:, g * HEAD_SIZE:(g + 1) * HEAD_SIZE]
        vg[g, c] = v_ref[:, g * HEAD_SIZE:(g + 1) * HEAD_SIZE]
    pl.semaphore_wait(barrier, n * tn - 1)

    def kv_copies(g, src, dst, slot):
        dev = {"ctx": dst}
        span = slice(g * HEAD_SIZE, (g + 1) * HEAD_SIZE)
        plan = [
            (k_ref.at[:, span], kg.at[g, src], k_send.at[g, slot], k_recv.at[g, src]),
            (v_ref.at[:, span], vg.at[g, src], v_send.at[g, slot], v_recv.at[g, src]),
        ]
        if g == 0:
            plan.insert(0, (cg.at[src], cg.at[src], c_send.at[slot], c_recv.at[src]))
        return [
            pltpu.make_async_remote_copy(
                src_ref=a, dst_ref=b, send_sem=x, recv_sem=y, device_id=dev, device_id_type=MESH
            )
            for a, b, x, y in plan
        ]

    def att_copy(s, g, d):
        return pltpu.make_async_remote_copy(
            src_ref=att.at[s, g], dst_ref=att.at[s, g],
            send_sem=att_send.at[d, s, g], recv_sem=att_recv.at[s, g],
            device_id={"ctx": c + 1 - 2 * d}, device_id_type=MESH,
        )

    def band(p):
        return pl.ds(p * piece, piece)

    def rs_copy(s, i, p):
        return pltpu.make_async_remote_copy(
            src_ref=part.at[s, i, band(p)], dst_ref=rs.at[s, t, band(p)],
            send_sem=rs_send.at[s, i, p], recv_sem=rs_recv.at[s, t, p],
            device_id={"tp": i}, device_id_type=MESH,
        )

    def rs_arrival(s, i, p):
        return pltpu.make_async_remote_copy(
            src_ref=part.at[s, i, band(p)], dst_ref=rs.at[s, i, band(p)],
            send_sem=rs_send.at[s, i, p], recv_sem=rs_recv.at[s, i, p],
            device_id={"tp": i}, device_id_type=MESH,
        )

    def fin_copy(s, p):
        return pltpu.make_async_remote_copy(
            src_ref=red.at[s, band(p)], dst_ref=fin.at[t, band(p)],
            send_sem=fin_send.at[s, p], recv_sem=fin_recv.at[t, p],
            device_id={"ctx": s, "tp": c}, device_id_type=MESH,
        )

    def fin_arrival(i, p):
        return pltpu.make_async_remote_copy(
            src_ref=red.at[0, band(p)], dst_ref=fin.at[i, band(p)],
            send_sem=fin_send.at[0, p], recv_sem=fin_recv.at[i, p],
            device_id={"ctx": t, "tp": i}, device_id_type=MESH,
        )

    def goes(s, d):
        if d == 0:
            return (s <= c) & (c < n - 1)
        return (s >= c) & (c > 0)

    for g in range(groups):
        for j in range(1, n):
            dst = lax.rem(c + n - j, n)
            for cp in kv_copies(g, c, dst, dst):
                cp.start()
    for i in range(tn):
        w_copy(i).start()
    res_copy.start()

    for g in range(groups):
        for h in range(per):
            col = (g * per + h) * HEAD_SIZE
            qs[g, h * rows:(h + 1) * rows, :] = q_ref[:, col:col + HEAD_SIZE]
    idcol = ids[...].T[:rows, :]
    tcol[...] = idcol[:, 2:3]
    qrow[...] = jnp.concatenate([idcol] * per, axis=0).T[0:8, :]

    for g in range(groups):
        for j in range(1, n):
            src = lax.rem(c + n - j, n)
            for cp in kv_copies(g, src, src, src):
                cp.wait_recv()
        if g == 0:
            for s in range(n):
                ids[s:s + 1, :] = cg[s, 0:1, :]
            columns = ids[...].T[:rows, :]
            for s in range(n):
                ccol[s] = columns[:, s:s + 1]

        def score_step(i, _):
            span = pl.ds(pl.multiple_of(i * lanes, 128), lanes)
            keys = kg[g].reshape(keys_all, HEAD_SIZE)
            vals = vg[g].reshape(keys_all, HEAD_SIZE)
            s = lax.dot_general(
                keys, qs[g, span, :], (((1,), (1,)), ((), ())), preferred_element_type=F32
            ) * scale
            cj = ccol[...].reshape(keys_all, 1)
            allowed = (cj <= qrow[0:1, span]) & (cj >= qrow[1:2, span])
            s = jnp.where(allowed, s, -1e30)
            top = jnp.max(s, axis=0, keepdims=True)
            p = jnp.where(allowed, jnp.exp(s - top), 0.0)
            den = jnp.sum(p, axis=0, keepdims=True)
            o = lax.dot_general(
                vals, p.astype(BF16), (((0,), (0,)), ((), ())), preferred_element_type=F32
            )
            ot[span, :] = (o / den).T.astype(BF16)
            return 0

        lax.fori_loop(0, per * rows // lanes, score_step, 0)
        for h in range(per):
            att[c, g, :, h * HEAD_SIZE:(h + 1) * HEAD_SIZE] = ot[h * rows:(h + 1) * rows, :]
        for d in range(2):
            @pl.when(goes(c, d))
            def _():
                att_copy(c, g, d).start()

    for i in range(tn):
        w_copy(i).wait()

    def column_of(j):
        if tn == 4:
            odd = lax.rem(t, 2)
            shift = jnp.where(
                j == 0, 2, jnp.where(j == 1, 3 - 2 * odd, jnp.where(j == 2, 1 + 2 * odd, 0))
            )
            return lax.rem(t + shift, tn)
        return lax.rem(t + 1 + j, tn)

    def project(s, side, g):
        def column(j, _):
            i = column_of(j)
            prod = jnp.dot(
                att[s, g], wv[i, g * half:(g + 1) * half, :], preferred_element_type=F32
            )
            if g > 0:
                prod = acc[side, i] + prod
            if g < groups - 1:
                acc[side, i] = prod
                return 0
            value = prod.astype(BF16)

            @pl.when(i == t)
            def _():
                rs[s, t] = value

            @pl.when(i != t)
            def _():
                part[s, i] = value

            if tn == 4:
                @pl.when(j == 1)
                def _():
                    for p in range(pieces):
                        rs_copy(s, column_of(0), p).start()
                        rs_copy(s, i, p).start()

                @pl.when(j == 2)
                def _():
                    for p in range(pieces):
                        rs_copy(s, i, p).start()
            else:
                @pl.when(i != t)
                def _():
                    for p in range(pieces):
                        rs_copy(s, i, p).start()

            return 0

        lax.fori_loop(0, tn, column, 0)

    def reduce_send(s):
        mine = (s == c) & (t == c)
        for p in range(pieces):
            for i in range(tn):
                @pl.when(t != i)
                def _():
                    rs_arrival(s, i, p).wait_recv()
            rng = slice(p * piece, (p + 1) * piece)
            total = None
            for i in range(tn):
                term = rs[s, i, rng, :].astype(F32)
                total = term if total is None else total + term
            summed = total.astype(BF16)

            @pl.when(mine)
            def _():
                fin[t, rng, :] = summed

            @pl.when(jnp.logical_not(mine))
            def _():
                red[s, rng, :] = summed
                fin_copy(s, p).start()

    def both_sides(k, act):
        def one(side, _):
            s = c + k * (2 * side - 1)

            @pl.when((s >= 0) & (s < n) & ((k > 0) | (side == 0)))
            def _():
                act(s, side)

            return 0

        lax.fori_loop(0, 2, one, 0)

    for g in range(groups):
        project(c, 0, g)

    def step(k, _):
        for g in range(groups):
            def take(s, side):
                att_copy(s, g, 0).wait_recv()
                for d in range(2):
                    @pl.when(goes(s, d))
                    def _():
                        att_copy(s, g, d).start()

            both_sides(k, take)
            both_sides(k, lambda s, side: project(s, side, g))
            if g == 0:
                both_sides(k - 1, lambda s, side: reduce_send(s))
        return 0

    lax.fori_loop(1, n, step, 0)
    both_sides(n - 1, lambda s, side: reduce_send(s))

    res_copy.wait()
    line = jnp.zeros((1, 128), F32)
    lane = lax.broadcasted_iota(jnp.int32, (piece, 128), 1)
    one = jnp.where(t == 0, 1.0, 0.0)
    for p in range(pieces):
        rng = slice(p * piece, (p + 1) * piece)
        score = jnp.zeros((piece, 1), F32)
        for i in range(tn):
            @pl.when(jnp.logical_not((c == t) & (t == i)))
            def _():
                fin_arrival(i, p).wait_recv()
            span = slice(i * cb, (i + 1) * cb)
            hidden = (resv[rng, span].astype(F32) + fin[i, rng, :].astype(F32)).astype(BF16)
            out_ref[rng, span] = hidden
            score = score + jnp.sum(
                hidden.astype(F32) * vh_ref[span].astype(F32).reshape(1, cb), axis=1, keepdims=True
            )
        turn = tcol[rng, :]
        terms = jnp.where(turn == lane, score, jnp.where(turn + 64 == lane, one, 0.0))
        line = line + jnp.sum(terms, axis=0, keepdims=True)
    me = c * tn + t
    tot[me] = line

    def tot_copy(j):
        other = lax.rem(me + j, n * tn)
        return pltpu.make_async_remote_copy(
            src_ref=tot.at[me], dst_ref=tot.at[me],
            send_sem=tot_send.at[other], recv_sem=tot_recv.at[me],
            device_id={"ctx": other // tn, "tp": lax.rem(other, tn)}, device_id_type=MESH,
        )

    def tot_arrival(j):
        other = lax.rem(me + j, n * tn)
        return pltpu.make_async_remote_copy(
            src_ref=tot.at[me], dst_ref=tot.at[other],
            send_sem=tot_send.at[other], recv_sem=tot_recv.at[other],
            device_id={"ctx": other // tn, "tp": lax.rem(other, tn)}, device_id_type=MESH,
        )

    def tot_start(j, _):
        tot_copy(j).start()
        return 0

    lax.fori_loop(1, n * tn, tot_start, 0)

    def drain(s, _):
        @pl.when(s != c)
        def _():
            for g in range(groups):
                for cp in kv_copies(g, c, s, s):
                    cp.wait_send()

        for d in range(2):
            @pl.when(goes(s, d))
            def _():
                for g in range(groups):
                    att_copy(s, g, d).wait_send()
        for i in range(tn):
            @pl.when(t != i)
            def _():
                for p in range(pieces):
                    rs_copy(s, i, p).wait_send()

        @pl.when(jnp.logical_not((s == c) & (t == c)))
        def _():
            for p in range(pieces):
                fin_copy(s, p).wait_send()

        return 0

    lax.fori_loop(0, n, drain, 0)

    def tot_wait(j, _):
        tot_arrival(j).wait_recv()
        tot_copy(j).wait_send()
        return 0

    lax.fori_loop(1, n * tn, tot_wait, 0)
    mean_ref[...] = jnp.sum(tot[...], axis=0)


def fused(
    n, tn, queries, keys, values, residual, out_weight, value_head, segment_ids, positions, turn_ids
):
    rows, width = queries.shape
    groups = keys.shape[1] // HEAD_SIZE
    per = width // keys.shape[1]
    cols = out_weight.shape[1]
    cb = cols // tn
    lanes = next(x for x in (384, 256, 128) if (per * rows) % x == 0)
    padded = -(-rows // 128) * 128
    pieces = 3 if rows % 48 == 0 else 1
    dims = (n, tn, rows, groups, per, cb, lanes, pieces)
    vmem = pl.BlockSpec(memory_space=pltpu.VMEM)
    hbm = pl.BlockSpec(memory_space=pl.ANY)
    dma = pltpu.SemaphoreType.DMA
    out, means = pl.pallas_call(
        functools.partial(kernel, dims),
        out_shape=(
            jax.ShapeDtypeStruct((rows, cols), BF16),
            jax.ShapeDtypeStruct((1, 128), F32),
        ),
        in_specs=[vmem] * 7 + [hbm] * 2,
        out_specs=(vmem, vmem),
        scratch_shapes=[
            pltpu.VMEM((groups, n, rows, HEAD_SIZE), BF16),
            pltpu.VMEM((groups, n, rows, HEAD_SIZE), BF16),
            pltpu.VMEM((n, 8, padded), jnp.int32),
            pltpu.VMEM((n, rows, 1), jnp.int32),
            pltpu.VMEM((128, padded), jnp.int32),
            pltpu.VMEM((rows, 1), jnp.int32),
            pltpu.VMEM((8, per * rows), jnp.int32),
            pltpu.VMEM((groups, per * rows, HEAD_SIZE), BF16),
            pltpu.VMEM((per * rows, HEAD_SIZE), BF16),
            pltpu.VMEM((n, groups, rows, per * HEAD_SIZE), BF16),
            pltpu.VMEM((tn, width, cb), BF16),
            pltpu.VMEM((2, tn, rows, cb), F32),
            pltpu.VMEM((n, tn, rows, cb), BF16),
            pltpu.VMEM((n, tn, rows, cb), BF16),
            pltpu.VMEM((n, rows, cb), BF16),
            pltpu.VMEM((tn, rows, cb), BF16),
            pltpu.VMEM((rows, cols), BF16),
            pltpu.VMEM((n * tn, 1, 128), F32),
            dma((groups, n)), dma((groups, n)), dma((n,)),
            dma((groups, n)), dma((groups, n)), dma((n,)),
            dma((2, n, groups)), dma((n, groups)),
            dma((n, tn, pieces)), dma((n, tn, pieces)),
            dma((n, pieces)), dma((tn, pieces)),
            dma((n * tn,)), dma((n * tn,)),
            dma((tn,)), dma(()),
        ],
        compiler_params=pltpu.CompilerParams(
            collective_id=0, has_side_effects=True, vmem_limit_bytes=56 * 1024 * 1024
        ),
    )(
        queries, keys, values, segment_ids, positions, turn_ids,
        value_head, residual, out_weight,
    )
    return out, means[0, :TURNS] / jnp.maximum(means[0, 64:64 + TURNS], 1.0)


def body(n, tn, *args):
    queries, weight = args[0], args[4]
    rows = queries.shape[0]
    fits = n == tn and n <= 128 and rows % 16 == 0 and weight.shape[1] % (128 * tn) == 0
    if fits:
        return fused(n, tn, *args)
    return shards(*args)


def solution(mesh):
    return jax.shard_map(
        functools.partial(body, mesh.shape["ctx"], mesh.shape["tp"]),
        mesh=mesh,
        in_specs=(
            P(("groups", "ctx"), "tp"),
            P(("groups", "ctx"), "tp"),
            P(("groups", "ctx"), "tp"),
            P(("groups", "ctx"), "tp"),
            P("tp", "ctx"),
            P("tp"),
            P(("groups", "ctx")),
            P(("groups", "ctx")),
            P(("groups", "ctx")),
        ),
        out_specs=(P(("groups", "ctx"), "tp"), P("groups")),
        check_vma=False,
    )
```
